32 devices in a mesh: segment: 2 (over core), tp: 8 (over z, y), dp: 2 (over x).
Axes of the slice: x: 2, y: 2, z: 4, core: 2. Of those that a mesh axis runs over, the one named last changes fastest.
Arguments:
- inputs: bfloat16 [1, 256, 6144], P(None, 'dp', 'tp'), parts along dimension 1, may hold values from -6 to 6
- norm_gain: float32 [2, 6144], P('segment'), may hold values from 0.1 to 1.9
- w_in: bfloat16 [2, 24576, 6144], P('segment', 'tp'), may hold values from -0.109375 to 0.109375
- b_in: float32 [2, 24576], P('segment', 'tp'), may hold values from -3 to 3
- w_out: bfloat16 [2, 6144, 24576], P('segment', 'tp'), may hold values from -0.0546875 to 0.0546875
- b_out: float32 [2, 6144], P('segment', 'tp'), may hold values from -3 to 3
Outputs:
- sections_out: bfloat16 [2, 1, 256, 6144], P('segment', None, 'dp', 'tp'), parts along dimension 2
The draws below stay inside these ranges and needn't reach their ends.
There are 2 independent parts, one for each index of `dp`. The reference program is written for one: setup_inputs(seed, part) draws one part's arguments, and reference() takes and returns one part's arrays. A program takes and returns all parts, laid end to end along the dimension named above; an argument that names none is the same for every part. Nothing has to cross between parts.
All inputs are finite; a program needn't handle non-finite values.
Results may differ from the reference program's by a relative error of at most 0.0058.
Values may be sent and summed in bfloat16 or wider, within the bound.
No kernel may reach another device: no remote copies, remote signals or barrier semaphores. Data moves between devices by JAX's collectives and lax.ppermute only.
A program may use at most 192 MiB of HBM per device.

```python
import jax
import jax.numpy as jnp
from jax import lax

D = 6144
FF = 24576
TOK = 128
MB = 1


def raised(result, rng, source, target, blocks, factor):
    def block_of(dim):
        return (jnp.arange(result.shape[dim]) // (result.shape[dim] // blocks)).reshape((-1,) + (1,) * (result.ndim - 1 - dim))

    near = jax.random.permutation(rng, blocks)[block_of(target)]
    other_side = (block_of(target) + blocks // 2) % blocks
    return jnp.where((block_of(source) == near) | (block_of(source) == other_side), factor * result, result)


def block_scale(own_key, extent, split, smallest, high):
    def one(axis_at, blocks):
        draws = jax.random.uniform(jax.random.fold_in(jax.random.fold_in(own_key, 6), axis_at), (blocks,), jnp.float32, smallest / len(split), high / len(split))
        return jnp.repeat(jnp.exp(draws), extent[axis_at] // blocks).reshape((-1,) + (1,) * (len(extent) - axis_at - 1))

    loudness = one(*split[0])
    for cut in split[1:]:
        loudness = loudness * one(*cut)
    return loudness


def normal_values(stream_key, shape, width, most, split=(), dtype=jnp.bfloat16):
    factor_of = block_scale(stream_key, shape, split, -0.22, 0.18) if split else 1.0
    drawn = jax.random.normal(stream_key, shape, jnp.float32) * width * factor_of
    return jnp.minimum(jnp.maximum(drawn, -most), most).astype(dtype)


def gaussian_with(rng, dims, scale, reach, shards, heavy, held_as=jnp.bfloat16):
    entries = scale * jax.random.normal(rng, dims, jnp.float32)
    if shards:
        entries = entries * block_scale(rng, dims, shards, -0.22, 0.18)
    return jnp.clip(raised(entries, jax.random.fold_in(rng, 3), *heavy), -reach, reach).astype(held_as)


def setup_inputs(seed: int = 0, part: int = 0) -> dict:
    arg_keys = jax.random.split(jax.random.key(seed), 7)
    part_splits = jax.random.split(jax.random.fold_in(arg_keys[6], part), 7)
    return {
        "inputs": normal_values(part_splits[0], (MB, TOK, D), 1.0, 6.0, ((2, 8),)),
        "norm_gain": jnp.clip(1.0 + 0.18 * jax.random.normal(arg_keys[1], (2, D), jnp.float32), 0.1, 1.9),
        "w_in": gaussian_with(arg_keys[2], (2, FF, D), D ** -0.5, 0.109375, ((0, 2), (1, 8)), (2, 1, 8, 2.0)),
        "b_in": normal_values(arg_keys[3], (2, FF), 0.5, 3.0, ((0, 2), (1, 8)), jnp.float32),
        "w_out": gaussian_with(arg_keys[4], (2, D, FF), FF ** -0.5, 0.0546875, ((0, 2), (1, 8)), (2, 1, 8, 2.0)),
        "b_out": normal_values(arg_keys[5], (2, D), 0.5, 3.0, ((0, 2), (1, 8)), jnp.float32),
    }


def section(rows_in, gain, w_first, b_first, w_second, b_second):
    values = rows_in.astype(jnp.float32)
    center = lax.optimization_barrier(jnp.mean(values, axis=1, keepdims=True))
    spread = lax.optimization_barrier(jnp.mean((values - center) ** 2, axis=1, keepdims=True))
    normed = ((values - center) * lax.rsqrt(spread + 1e-05) * gain).astype(jnp.bfloat16)
    pre = jnp.dot(normed, w_first.T, preferred_element_type=jnp.float32) + b_first
    hidden = jax.nn.gelu(pre, approximate=True).astype(jnp.bfloat16)
    branch = jnp.dot(hidden, w_second.T, preferred_element_type=jnp.float32) + b_second
    return (values + branch).astype(jnp.bfloat16)

def reference(inputs, norm_gain, w_in, b_in, w_out, b_out):
    first = lax.map(lambda m: section(m, norm_gain[0], w_in[0], b_in[0], w_out[0], b_out[0]), inputs)
    second = lax.map(lambda m: section(m, norm_gain[1], w_in[1], b_in[1], w_out[1], b_out[1]), first)
    return jnp.stack([first, second])
```

```python
import functools

import jax
import jax.numpy as jnp
import numpy as np
from jax import lax
from jax.experimental import pallas as pl
from jax.experimental.pallas import tpu as pltpu
from jax.sharding import PartitionSpec as P

MIB = 1024 * 1024
VM = pl.BlockSpec(memory_space=pltpu.VMEM)
SM = pl.BlockSpec(memory_space=pltpu.SMEM)
ANY = pl.BlockSpec(memory_space=pl.ANY)


def shifted(value, axis, steps):
    count = lax.axis_size(axis)
    first, last = (max(0, -steps), min(count, count - steps))
    return lax.ppermute(value, axis, [(source, source + steps) for source in range(first, last)])


def contract(left, right):
    return lax.dot_general(
        left, right, (((1,), (1,)), ((), ())), preferred_element_type=jnp.float32
    )


def plain_section(local, gain, w_first, b_first, w_second, b_second):
    whole = lax.all_gather(local, "tp", axis=1, tiled=True)
    values = whole.astype(jnp.float32)
    center = jnp.mean(values, axis=1, keepdims=True)
    spread = jnp.mean((values - center) ** 2, axis=1, keepdims=True)
    normed = ((values - center) * lax.rsqrt(spread + 1e-05) * gain).astype(jnp.bfloat16)
    pre = contract(normed, w_first) + b_first
    hidden = jax.nn.gelu(pre, approximate=True).astype(jnp.bfloat16)
    branch = contract(lax.all_gather(hidden, "tp", axis=1, tiled=True), w_second)
    return (local.astype(jnp.float32) + branch + b_second).astype(jnp.bfloat16)


def plain_shards(inputs, norm_gain, w_in, b_in, w_out, b_out):
    batches, tok_rows, width = inputs.shape
    first_segment = lax.axis_index("segment") == 0
    incoming = jnp.zeros((tok_rows, width), jnp.bfloat16)
    results = []
    for tick in range(batches + 1):
        own = inputs[min(tick, batches - 1)]
        current = jnp.where(first_segment, own, incoming)
        result = plain_section(current, norm_gain[0], w_in[0], b_in[0], w_out[0], b_out[0])
        results.append(result)
        if tick < batches:
            incoming = shifted(result, "segment", 1)
    early = jnp.stack(results[:batches])
    late = jnp.stack(results[1:])
    chosen = jnp.where(first_segment, early, late)
    return chosen.reshape(1, batches, tok_rows, width)


def pallas(kernel, outs, specs, out_specs, scratch=(), limit=28, flops=0, moved=0):
    return pl.pallas_call(
        kernel,
        out_shape=outs,
        in_specs=specs,
        out_specs=out_specs,
        scratch_shapes=list(scratch),
        compiler_params=pltpu.CompilerParams(vmem_limit_bytes=limit * MIB),
        cost_estimate=pl.CostEstimate(flops=flops, bytes_accessed=moved, transcendentals=0),
    )


def normalize(pieces, spots, gain_ref, out_ref):
    width = out_ref.shape[0]
    total = 0.0
    for ref in pieces:
        total = total + jnp.sum(ref[...].astype(jnp.float32), axis=0, keepdims=True)
    center = total / width
    square = 0.0
    for ref in pieces:
        square = square + jnp.sum((ref[...].astype(jnp.float32) - center) ** 2, axis=0, keepdims=True)
    scale = lax.rsqrt(square / width + 1e-05)
    for ref, spot in zip(pieces, spots):
        rows = pl.ds(pl.multiple_of(spot, 64), ref.shape[0])
        value = (ref[...].astype(jnp.float32) - center) * scale * gain_ref[rows, :]
        out_ref[rows, :] = value.astype(jnp.bfloat16)


def first_kernel(offset, tile, slots, layout, info_ref, bias_ref, w_ref, *refs):
    out_ref, buf, sems = refs[-3:]
    rows = out_ref.shape[0]
    steps = rows // tile

    def copy(step, slot):
        start = pl.multiple_of(offset + step * tile, tile)
        return pltpu.make_async_copy(w_ref.at[0, pl.ds(start, tile), :], buf.at[slot], sems.at[slot])

    for step in range(min(slots, steps)):
        copy(step, step).start()
    if layout is None:
        normed_ref = refs[0]
    else:
        gain_ref, pieces, normed_ref = refs[0], refs[1:-4], refs[-4]
        part, half, places = layout
        seg = info_ref[0]
        spots = [info_ref[1 + k] * part + row + seg * half for k, row in places]
        spots += [info_ref[1 + k] * part + row + (1 - seg) * half for k, row in places]
        normalize(pieces, spots, gain_ref, normed_ref)

    def body(step, carry):
        slot = lax.rem(step, slots)
        copy(step, slot).wait()
        at = pl.multiple_of(step * tile, tile)
        pre = jnp.dot(buf[slot], normed_ref[...], preferred_element_type=jnp.float32)
        pre = pre + bias_ref[pl.ds(pl.multiple_of(offset + at, tile), tile), :]
        out_ref[pl.ds(at, tile), :] = jax.nn.gelu(pre, approximate=True).astype(jnp.bfloat16)

        @pl.when(step + slots < steps)
        def _():
            copy(step + slots, slot).start()

        return carry

    lax.fori_loop(0, steps, body, 0)


def first_matmul(info, bias, w, offset, rows, normed=None, gain=None, pieces=None, layout=None):
    tile = 256
    slots = min(4, rows // tile)
    width, tokens = w.shape[2], bias.shape[1]
    out = jax.ShapeDtypeStruct((rows, tokens), jnp.bfloat16)
    scratch = [pltpu.VMEM((slots, tile, width), jnp.bfloat16), pltpu.SemaphoreType.DMA((slots,))]
    cost = dict(flops=2 * rows * width * tokens, moved=2 * rows * width)
    if pieces is None:
        kernel = functools.partial(first_kernel, offset, tile, slots, None)
        return pallas(kernel, out, [SM, VM, ANY, VM], VM, scratch, **cost)(info, bias, w, normed)
    kernel = functools.partial(first_kernel, offset, tile, slots, layout)
    outs = [jax.ShapeDtypeStruct((width, tokens), jnp.bfloat16), out]
    call = pallas(kernel, outs, [SM, VM, ANY, VM] + [VM] * len(pieces), [VM, VM], scratch, **cost)
    return call(info, bias, w, gain, *pieces)


def pick_kernel(phase, info_ref, here_ref, crossed_ref, out_ref):
    @pl.when(info_ref[0] == phase)
    def _():
        out_ref[...] = here_ref[...]

    @pl.when(info_ref[0] != phase)
    def _():
        out_ref[...] = crossed_ref[...]


def pick(phase, info, here, crossed):
    out = jax.ShapeDtypeStruct(here.shape, here.dtype)
    return pallas(functools.partial(pick_kernel, phase), out, [SM, VM, VM], VM, limit=8)(info, here, crossed)


def relay_kernel(info_ref, kept_ref, swapped_ref, out_ref, own_ref):
    half = own_ref.shape[0]

    @pl.when(info_ref[0] == 0)
    def _():
        out_ref[...] = kept_ref[...]
        own_ref[...] = kept_ref[:half]

    @pl.when(info_ref[0] != 0)
    def _():
        out_ref[...] = swapped_ref[...]
        own_ref[...] = swapped_ref[half:]


def relay(info, kept, swapped):
    half = (kept.shape[0] // 2, kept.shape[1])
    outs = [jax.ShapeDtypeStruct(kept.shape, kept.dtype), jax.ShapeDtypeStruct(half, kept.dtype)]
    return pallas(relay_kernel, outs, [SM, VM, VM], [VM, VM], limit=8)(info, kept, swapped)


def halve_kernel(front_ref, back_ref, lower_ref, upper_ref):
    mid = lower_ref.shape[0]
    lower_ref[...] = front_ref[:mid]
    upper_ref[...] = back_ref[mid:]


def halve(front, back):
    mid = front.shape[0] // 2
    outs = [
        jax.ShapeDtypeStruct((mid, front.shape[1]), front.dtype),
        jax.ShapeDtypeStruct((front.shape[0] - mid, front.shape[1]), front.dtype),
    ]
    return pallas(halve_kernel, outs, [VM, VM], [VM, VM], limit=8)(front, back)


def second_kernel(places, first, ending, *refs):
    count = len(places)
    info_ref, w_ref = refs[:2]
    pieces, refs = refs[2 : 2 + count], refs[2 + count :]
    buf, joined, sems = refs[-3:]
    refs = refs[:-3]
    if not first:
        acc_ref, refs = refs[0], refs[1:]
    depth, tile = w_ref.shape[1], 256
    copies = {}
    for t in range(depth // tile):
        at = 0
        for i, (k, scale, row) in enumerate(places):
            rows = pieces[i].shape[0]
            columns = pl.ds(pl.multiple_of(info_ref[1 + k] * scale + row, 128), rows)
            copies[t, i] = pltpu.make_async_copy(
                w_ref.at[0, pl.ds(t * tile, tile), columns],
                buf.at[pl.ds(t * tile, tile), pl.ds(at, rows)],
                sems.at[t, i],
            )
            copies[t, i].start()
            at += rows
    at = 0
    for ref in pieces:
        joined[pl.ds(at, ref.shape[0]), :] = ref[...]
        at += ref.shape[0]
    for t in range(depth // tile):
        for i in range(count):
            copies[t, i].wait()
        own = pl.ds(t * tile, tile)
        acc = jnp.dot(buf[own, :], joined[...], preferred_element_type=jnp.float32)
        if not first:
            acc = acc_ref[own, :] + acc
        if not ending:
            refs[0][own, :] = acc
            continue
        local_ref, bias_ref = refs[:2]
        result = local_ref[own, :].astype(jnp.float32) + (acc + bias_ref[own, :])
        if ending == 1:
            refs[2][own, :] = result.astype(jnp.bfloat16)
        else:
            early_ref, out_ref = refs[2:]
            result = jnp.where(info_ref[0] == 0, early_ref[own, :].astype(jnp.float32), result)
            out_ref[:, own] = result.T.astype(jnp.bfloat16)


def second_matmul(info, acc, pieces, places, w, ends=()):
    depth, tokens = w.shape[1], pieces[0].shape[1]
    total = sum(piece.shape[0] for piece in pieces)
    ending = max(0, len(ends) - 1)
    args = [info, w, *pieces] + ([] if acc is None else [acc]) + list(ends)
    if ending == 2:
        out = jax.ShapeDtypeStruct((tokens, depth), jnp.bfloat16)
    else:
        out = jax.ShapeDtypeStruct((depth, tokens), jnp.bfloat16 if ending else jnp.float32)
    scratch = [
        pltpu.VMEM((depth, total), jnp.bfloat16),
        pltpu.VMEM((total, tokens), jnp.bfloat16),
        pltpu.SemaphoreType.DMA((depth // 256, len(pieces))),
    ]
    kernel = functools.partial(second_kernel, places, acc is None, ending)
    cost = dict(flops=2 * depth * total * tokens, moved=2 * depth * total)
    return pallas(kernel, out, [SM, ANY] + [VM] * (len(args) - 2), VM, scratch, **cost)(*args)


def ring_shards(ring, inputs, norm_gain, w_in, b_in, w_out, b_out):
    n = len(ring)
    last = n // 2
    tokens, part = inputs.shape[1:]
    half = part // 2
    width = norm_gain.shape[1]
    hidden = w_in.shape[1]
    side = hidden // 2
    seg = lax.axis_index("segment")
    place = {device: at for at, device in enumerate(ring)}
    behind = np.array([[ring[(place[t] - k) % n] for k in range(n)] for t in range(n)], np.int32)
    owner = jnp.asarray(behind)[lax.axis_index("tp")]
    info = jnp.concatenate([seg.reshape(1).astype(jnp.int32), owner])

    def hop(value, steps):
        return lax.ppermute(value, "tp", [(ring[at], ring[(at + steps) % n]) for at in range(n)])

    def swap(value):
        return lax.ppermute(value, "segment", [(0, 1), (1, 0)])

    def after(values, *others):
        return lax.optimization_barrier((*values, *others))[: len(values)]

    local = inputs[0].T
    own = lax.dynamic_slice_in_dim(inputs[0], seg * half, half, 1).T
    gain = jnp.broadcast_to(norm_gain[0][:, None], (width, tokens))
    bias_in = jnp.broadcast_to(b_in[0][:, None], (hidden, tokens))
    bias_out = jnp.broadcast_to(b_out[0][:, None], (part, tokens))

    mid = half // 2
    x_places = [(0, 0)] + [(k, 0) for step in range(1, last) for k in (step, n - step)] + [(last, 0), (last, mid)]

    early = None
    for phase in range(2):
        front = back = own
        mine, theirs = [own], [swap(own)]
        for step in range(1, last + 1):
            if step == last:
                front, back = halve(front, back)
            front, back = hop(front, 1), hop(back, -1)
            if phase == 0 and step == 1:
                front, back, info, gain, bias_in, bias_out, local = lax.optimization_barrier(
                    (front, back, info, gain, bias_in, bias_out, local)
                )
            mine += [front, back]
            theirs += [swap(front), swap(back)]
        normed, other = first_matmul(
            info, bias_in, w_in, side, side, gain=gain, pieces=mine + theirs, layout=(part, half, x_places)
        )
        crossed = swap(other)
        here = first_matmul(info, bias_in, w_in, 0, side, normed=normed)
        front = back = pick(phase, info, here, crossed)
        done = [(here, other)]
        acc = None
        ready = [(0, hidden, 0), (0, hidden, side)], [here, other]
        for step in range(1, last + 1):
            if step == last:
                front, back = halve(front, back)
            if acc is not None:
                front, back = after((front, back), acc)
            front, back = hop(front, 1), hop(back, -1)
            acc = second_matmul(info, acc, ready[1], ready[0], w_out)
            at = side // 2 if step == last else 0
            k = (step, n - step)
            ready = (
                [(k[0], hidden, 0), (k[1], hidden, at), (k[0], hidden, side), (k[1], hidden, side + at)],
                [front, back, swap(front), swap(back)],
            )
        acc = second_matmul(info, acc, ready[1][:2], ready[0][:2], w_out)
        ends = [local, bias_out] + ([] if early is None else [early])
        result = second_matmul(info, acc, ready[1][2:], ready[0][2:], w_out, ends)
        if phase == 0:
            early = result
            local, own = relay(info, early, swap(early))
    return result.reshape(1, 1, tokens, part)


def snake(mesh):
    n = mesh.shape["tp"]
    return [2 * at for at in range(n // 2)] + [2 * at + 1 for at in reversed(range(n // 2))]


def solution(mesh):
    def shards(inputs, norm_gain, w_in, b_in, w_out, b_out):
        small = mesh.shape["tp"] == 8 and mesh.shape["segment"] == 2 and inputs.shape[0] == 1
        if small and inputs.shape[2] % 512 == 0 or small and inputs.shape[2] % 768 == 0:
            return ring_shards(snake(mesh), inputs, norm_gain, w_in, b_in, w_out, b_out)
        return plain_shards(inputs, norm_gain, w_in, b_in, w_out, b_out)

    return jax.shard_map(
        shards,
        mesh=mesh,
        in_specs=(
            P(None, "dp", "tp"),
            P("segment", None),
            P("segment", "tp", None),
            P("segment", "tp"),
            P("segment", "tp", None),
            P("segment", "tp"),
        ),
        out_specs=P("segment", None, "dp", "tp"),
        check_vma=False,
    )
```

```python
import functools

import jax
import jax.numpy as jnp
import numpy as np
from jax import lax
from jax.experimental import pallas as pl
from jax.experimental.pallas import tpu as pltpu
from jax.sharding import PartitionSpec as P

MIB = 1024 * 1024
VM = pl.BlockSpec(memory_space=pltpu.VMEM)
SM = pl.BlockSpec(memory_space=pltpu.SMEM)
ANY = pl.BlockSpec(memory_space=pl.ANY)


def shifted(value, axis, steps):
    count = lax.axis_size(axis)
    first, last = (max(0, -steps), min(count, count - steps))
    return lax.ppermute(value, axis, [(source, source + steps) for source in range(first, last)])


def contract(left, right):
    return lax.dot_general(
        left, right, (((1,), (1,)), ((), ())), preferred_element_type=jnp.float32
    )


def plain_section(local, gain, w_first, b_first, w_second, b_second):
    whole = lax.all_gather(local, "tp", axis=1, tiled=True)
    values = whole.astype(jnp.float32)
    center = jnp.mean(values, axis=1, keepdims=True)
    spread = jnp.mean((values - center) ** 2, axis=1, keepdims=True)
    normed = ((values - center) * lax.rsqrt(spread + 1e-05) * gain).astype(jnp.bfloat16)
    pre = contract(normed, w_first) + b_first
    hidden = jax.nn.gelu(pre, approximate=True).astype(jnp.bfloat16)
    branch = contract(lax.all_gather(hidden, "tp", axis=1, tiled=True), w_second)
    return (local.astype(jnp.float32) + branch + b_second).astype(jnp.bfloat16)


def plain_shards(inputs, norm_gain, w_in, b_in, w_out, b_out):
    batches, tok_rows, width = inputs.shape
    first_segment = lax.axis_index("segment") == 0
    incoming = jnp.zeros((tok_rows, width), jnp.bfloat16)
    results = []
    for tick in range(batches + 1):
        own = inputs[min(tick, batches - 1)]
        current = jnp.where(first_segment, own, incoming)
        result = plain_section(current, norm_gain[0], w_in[0], b_in[0], w_out[0], b_out[0])
        results.append(result)
        if tick < batches:
            incoming = shifted(result, "segment", 1)
    early = jnp.stack(results[:batches])
    late = jnp.stack(results[1:])
    chosen = jnp.where(first_segment, early, late)
    return chosen.reshape(1, batches, tok_rows, width)


def pallas(kernel, outs, specs, out_specs, scratch=(), limit=28, flops=0, moved=0):
    return pl.pallas_call(
        kernel,
        out_shape=outs,
        in_specs=specs,
        out_specs=out_specs,
        scratch_shapes=list(scratch),
        compiler_params=pltpu.CompilerParams(vmem_limit_bytes=limit * MIB),
        cost_estimate=pl.CostEstimate(flops=flops, bytes_accessed=moved, transcendentals=0),
    )


def normalize(pieces, spots, gain_ref, out_ref):
    width = out_ref.shape[0]
    total = 0.0
    for ref in pieces:
        total = total + jnp.sum(ref[...].astype(jnp.float32), axis=0, keepdims=True)
    center = total / width
    square = 0.0
    for ref in pieces:
        square = square + jnp.sum((ref[...].astype(jnp.float32) - center) ** 2, axis=0, keepdims=True)
    scale = lax.rsqrt(square / width + 1e-05)
    for ref, spot in zip(pieces, spots):
        rows = pl.ds(pl.multiple_of(spot, 64), ref.shape[0])
        value = (ref[...].astype(jnp.float32) - center) * scale * gain_ref[rows, :]
        out_ref[rows, :] = value.astype(jnp.bfloat16)


def first_kernel(offset, tile, slots, layout, info_ref, bias_ref, w_ref, *refs):
    out_ref, buf, sems = refs[-3:]
    rows = out_ref.shape[0]
    steps = rows // tile

    def copy(step, slot):
        start = pl.multiple_of(offset + step * tile, tile)
        return pltpu.make_async_copy(w_ref.at[0, pl.ds(start, tile), :], buf.at[slot], sems.at[slot])

    for step in range(min(slots, steps)):
        copy(step, step).start()
    if layout is None:
        normed_ref = refs[0]
    else:
        gain_ref, pieces, normed_ref = refs[0], refs[1:-4], refs[-4]
        part, half, places = layout
        seg = info_ref[0]
        spots = [info_ref[1 + k] * part + row + seg * half for k, row in places]
        spots += [info_ref[1 + k] * part + row + (1 - seg) * half for k, row in places]
        normalize(pieces, spots, gain_ref, normed_ref)

    def body(step, carry):
        slot = lax.rem(step, slots)
        copy(step, slot).wait()
        at = pl.multiple_of(step * tile, tile)
        pre = jnp.dot(buf[slot], normed_ref[...], preferred_element_type=jnp.float32)
        pre = pre + bias_ref[pl.ds(pl.multiple_of(offset + at, tile), tile), :]
        out_ref[pl.ds(at, tile), :] = jax.nn.gelu(pre, approximate=True).astype(jnp.bfloat16)

        @pl.when(step + slots < steps)
        def _():
            copy(step + slots, slot).start()

        return carry

    lax.fori_loop(0, steps, body, 0)


def first_matmul(info, bias, w, offset, rows, normed=None, gain=None, pieces=None, layout=None):
    tile = 256
    slots = min(6, rows // tile)
    width, tokens = w.shape[2], bias.shape[1]
    out = jax.ShapeDtypeStruct((rows, tokens), jnp.bfloat16)
    scratch = [pltpu.VMEM((slots, tile, width), jnp.bfloat16), pltpu.SemaphoreType.DMA((slots,))]
    cost = dict(flops=2 * rows * width * tokens, moved=2 * rows * width)
    if pieces is None:
        kernel = functools.partial(first_kernel, offset, tile, slots, None)
        return pallas(kernel, out, [SM, VM, ANY, VM], VM, scratch, **cost)(info, bias, w, normed)
    kernel = functools.partial(first_kernel, offset, tile, slots, layout)
    outs = [jax.ShapeDtypeStruct((width, tokens), jnp.bfloat16), out]
    call = pallas(kernel, outs, [SM, VM, ANY, VM] + [VM] * len(pieces), [VM, VM], scratch, **cost)
    return call(info, bias, w, gain, *pieces)


def pick_kernel(phase, info_ref, here_ref, crossed_ref, out_ref):
    @pl.when(info_ref[0] == phase)
    def _():
        out_ref[...] = here_ref[...]

    @pl.when(info_ref[0] != phase)
    def _():
        out_ref[...] = crossed_ref[...]


def pick(phase, info, here, crossed):
    out = jax.ShapeDtypeStruct(here.shape, here.dtype)
    return pallas(functools.partial(pick_kernel, phase), out, [SM, VM, VM], VM, limit=8)(info, here, crossed)


def relay_kernel(info_ref, kept_ref, swapped_ref, out_ref, own_ref):
    half = own_ref.shape[0]

    @pl.when(info_ref[0] == 0)
    def _():
        out_ref[...] = kept_ref[...]
        own_ref[...] = kept_ref[:half]

    @pl.when(info_ref[0] != 0)
    def _():
        out_ref[...] = swapped_ref[...]
        own_ref[...] = swapped_ref[half:]


def relay(info, kept, swapped):
    half = (kept.shape[0] // 2, kept.shape[1])
    outs = [jax.ShapeDtypeStruct(kept.shape, kept.dtype), jax.ShapeDtypeStruct(half, kept.dtype)]
    return pallas(relay_kernel, outs, [SM, VM, VM], [VM, VM], limit=8)(info, kept, swapped)


def halve_kernel(front_ref, back_ref, lower_ref, upper_ref):
    mid = lower_ref.shape[0]
    lower_ref[...] = front_ref[:mid]
    upper_ref[...] = back_ref[mid:]


def halve(front, back):
    mid = front.shape[0] // 2
    outs = [
        jax.ShapeDtypeStruct((mid, front.shape[1]), front.dtype),
        jax.ShapeDtypeStruct((front.shape[0] - mid, front.shape[1]), front.dtype),
    ]
    return pallas(halve_kernel, outs, [VM, VM], [VM, VM], limit=8)(front, back)


def second_kernel(places, first, ending, *refs):
    count = len(places)
    info_ref, w_ref = refs[:2]
    pieces, refs = refs[2 : 2 + count], refs[2 + count :]
    buf, joined, sems = refs[-3:]
    refs = refs[:-3]
    if not first:
        acc_ref, refs = refs[0], refs[1:]
    depth, tile = w_ref.shape[1], 256

    def tile_copies(t):
        at = 0
        for i, (k, scale, row) in enumerate(places):
            rows = pieces[i].shape[0]
            down = pl.ds(pl.multiple_of(t * tile, tile), tile)
            columns = pl.ds(pl.multiple_of(info_ref[1 + k] * scale + row, 128), rows)
            yield pltpu.make_async_copy(w_ref.at[0, down, columns], buf.at[down, pl.ds(at, rows)], sems.at[t, i])
            at += rows

    def start(t, carry):
        for copy in tile_copies(t):
            copy.start()
        return carry

    lax.fori_loop(0, depth // tile, start, 0)
    at = 0
    for ref in pieces:
        joined[pl.ds(at, ref.shape[0]), :] = ref[...]
        at += ref.shape[0]

    def body(t, carry):
        for copy in tile_copies(t):
            copy.wait()
        own = pl.ds(pl.multiple_of(t * tile, tile), tile)
        acc = jnp.dot(buf[own, :], joined[...], preferred_element_type=jnp.float32)
        if not first:
            acc = acc_ref[own, :] + acc
        if not ending:
            refs[0][own, :] = acc
            return carry
        local_ref, bias_ref = refs[:2]
        result = local_ref[own, :].astype(jnp.float32) + (acc + bias_ref[own, :])
        if ending == 1:
            refs[2][own, :] = result.astype(jnp.bfloat16)
        else:
            early_ref, out_ref = refs[2:]
            rounded = result.astype(jnp.bfloat16).astype(jnp.float32)
            result = jnp.where(info_ref[0] == 0, early_ref[own, :].astype(jnp.float32), rounded)
            out_ref[:, own] = result.T.astype(jnp.bfloat16)
        return carry

    lax.fori_loop(0, depth // tile, body, 0)


def second_matmul(info, acc, pieces, places, w, ends=()):
    depth, tokens = w.shape[1], pieces[0].shape[1]
    total = sum(piece.shape[0] for piece in pieces)
    ending = max(0, len(ends) - 1)
    args = [info, w, *pieces] + ([] if acc is None else [acc]) + list(ends)
    if ending == 2:
        out = jax.ShapeDtypeStruct((tokens, depth), jnp.bfloat16)
    else:
        out = jax.ShapeDtypeStruct((depth, tokens), jnp.bfloat16 if ending else jnp.float32)
    scratch = [
        pltpu.VMEM((depth, total), jnp.bfloat16),
        pltpu.VMEM((total, tokens), jnp.bfloat16),
        pltpu.SemaphoreType.DMA((depth // 256, len(pieces))),
    ]
    kernel = functools.partial(second_kernel, places, acc is None, ending)
    cost = dict(flops=2 * depth * total * tokens, moved=2 * depth * total)
    return pallas(kernel, out, [SM, ANY] + [VM] * (len(args) - 2), VM, scratch, **cost)(*args)


def ring_shards(ring, inputs, norm_gain, w_in, b_in, w_out, b_out):
    n = len(ring)
    last = n // 2
    tokens, part = inputs.shape[1:]
    half = part // 2
    width = norm_gain.shape[1]
    hidden = w_in.shape[1]
    side = hidden // 2
    seg = lax.axis_index("segment")
    place = {device: at for at, device in enumerate(ring)}
    behind = np.array([[ring[(place[t] - k) % n] for k in range(n)] for t in range(n)], np.int32)
    owner = jnp.asarray(behind)[lax.axis_index("tp")]
    info = jnp.concatenate([seg.reshape(1).astype(jnp.int32), owner])

    def hop(value, steps):
        return lax.ppermute(value, "tp", [(ring[at], ring[(at + steps) % n]) for at in range(n)])

    def swap(value):
        return lax.ppermute(value, "segment", [(0, 1), (1, 0)])

    local = inputs[0].T
    own = lax.dynamic_slice_in_dim(inputs[0], seg * half, half, 1).T
    gain = jnp.broadcast_to(norm_gain[0][:, None], (width, tokens))
    bias_in = jnp.broadcast_to(b_in[0][:, None], (hidden, tokens))
    bias_out = jnp.broadcast_to(b_out[0][:, None], (part, tokens))

    mid = half // 2
    x_places = [(0, 0)] + [(k, 0) for step in range(1, last) for k in (step, n - step)] + [(last, 0), (last, mid)]

    early = None
    for phase in range(2):
        front = back = own
        mine, theirs = [own], [swap(own)]
        for step in range(1, last + 1):
            if step == last:
                front, back = halve(front, back)
            front, back = hop(front, 1), hop(back, -1)
            if phase == 0 and step == 1:
                front, back, info, local = lax.optimization_barrier((front, back, info, local))
            if phase == 0 and step == 2:
                front, back, gain = lax.optimization_barrier((front, back, gain))
            if phase == 0 and step == 3:
                front, back, bias_in, bias_out = lax.optimization_barrier((front, back, bias_in, bias_out))
            mine += [front, back]
            theirs += [swap(front), swap(back)]
        normed, other = first_matmul(
            info, bias_in, w_in, side, side, gain=gain, pieces=mine + theirs, layout=(part, half, x_places)
        )
        crossed = swap(other)
        here = first_matmul(info, bias_in, w_in, 0, side, normed=normed)
        front = back = pick(phase, info, here, crossed)
        acc = None
        places, pieces = [(0, hidden, 0), (0, hidden, side)], [here, other]
        for step in range(1, last + 1):
            if step == last:
                front, back = halve(front, back)
            front, back = hop(front, 1), hop(back, -1)
            acc = second_matmul(info, acc, pieces, places, w_out)
            front, back, acc = lax.optimization_barrier((front, back, acc))
            at = side // 2 if step == last else 0
            places = [(step, hidden, 0), (n - step, hidden, at), (step, hidden, side), (n - step, hidden, side + at)]
            pieces = [front, back, swap(front), swap(back)]
        acc = second_matmul(info, acc, pieces[:2], places[:2], w_out)
        ends = [local, bias_out] + ([] if early is None else [early])
        result = second_matmul(info, acc, pieces[2:], places[2:], w_out, ends)
        if phase == 0:
            early = result
            local, own = relay(info, early, swap(early))
    return result.reshape(1, 1, tokens, part)


def snake(mesh):
    n = mesh.shape["tp"]
    return [2 * at for at in range(n // 2)] + [2 * at + 1 for at in reversed(range(n // 2))]


def solution(mesh):
    def shards(inputs, norm_gain, w_in, b_in, w_out, b_out):
        small = mesh.shape["tp"] == 8 and mesh.shape["segment"] == 2 and inputs.shape[0] == 1
        if small and inputs.shape[2] % 512 == 0 or small and inputs.shape[2] % 768 == 0:
            return ring_shards(snake(mesh), inputs, norm_gain, w_in, b_in, w_out, b_out)
        return plain_shards(inputs, norm_gain, w_in, b_in, w_out, b_out)

    return jax.shard_map(
        shards,
        mesh=mesh,
        in_specs=(
            P(None, "dp", "tp"),
            P("segment", None),
            P("segment", "tp", None),
            P("segment", "tp"),
            P("segment", "tp", None),
            P("segment", "tp"),
        ),
        out_specs=P("segment", None, "dp", "tp"),
        check_vma=False,
    )
```

```python
import functools

import jax
import jax.numpy as jnp
import numpy as np
from jax import lax
from jax.experimental import pallas as pl
from jax.experimental.pallas import tpu as pltpu
from jax.sharding import PartitionSpec as P

MIB = 1024 * 1024
VM = pl.BlockSpec(memory_space=pltpu.VMEM)
SM = pl.BlockSpec(memory_space=pltpu.SMEM)
ANY = pl.BlockSpec(memory_space=pl.ANY)
CHUNKS = 1


def shifted(value, axis, steps):
    count = lax.axis_size(axis)
    first, last = (max(0, -steps), min(count, count - steps))
    return lax.ppermute(value, axis, [(source, source + steps) for source in range(first, last)])


def contract(left, right):
    return lax.dot_general(
        left, right, (((1,), (1,)), ((), ())), preferred_element_type=jnp.float32
    )


def plain_section(local, gain, w_first, b_first, w_second, b_second):
    whole = lax.all_gather(local, "tp", axis=1, tiled=True)
    values = whole.astype(jnp.float32)
    center = jnp.mean(values, axis=1, keepdims=True)
    spread = jnp.mean((values - center) ** 2, axis=1, keepdims=True)
    normed = ((values - center) * lax.rsqrt(spread + 1e-05) * gain).astype(jnp.bfloat16)
    pre = contract(normed, w_first) + b_first
    hidden = jax.nn.gelu(pre, approximate=True).astype(jnp.bfloat16)
    branch = contract(lax.all_gather(hidden, "tp", axis=1, tiled=True), w_second)
    return (local.astype(jnp.float32) + branch + b_second).astype(jnp.bfloat16)


def plain_shards(inputs, norm_gain, w_in, b_in, w_out, b_out):
    batches, tok_rows, width = inputs.shape
    first_segment = lax.axis_index("segment") == 0
    incoming = jnp.zeros((tok_rows, width), jnp.bfloat16)
    results = []
    for tick in range(batches + 1):
        own = inputs[min(tick, batches - 1)]
        current = jnp.where(first_segment, own, incoming)
        result = plain_section(current, norm_gain[0], w_in[0], b_in[0], w_out[0], b_out[0])
        results.append(result)
        if tick < batches:
            incoming = shifted(result, "segment", 1)
    early = jnp.stack(results[:batches])
    late = jnp.stack(results[1:])
    chosen = jnp.where(first_segment, early, late)
    return chosen.reshape(1, batches, tok_rows, width)


def pallas(kernel, outs, specs, out_specs, scratch=(), limit=28, flops=0, moved=0):
    return pl.pallas_call(
        kernel,
        out_shape=outs,
        in_specs=specs,
        out_specs=out_specs,
        scratch_shapes=list(scratch),
        compiler_params=pltpu.CompilerParams(vmem_limit_bytes=limit * MIB),
        cost_estimate=pl.CostEstimate(flops=flops, bytes_accessed=moved, transcendentals=0),
    )


def normalize(pieces, spots, gain_ref, out_ref):
    width = out_ref.shape[0]
    total = 0.0
    for ref in pieces:
        total = total + jnp.sum(ref[...].astype(jnp.float32), axis=0, keepdims=True)
    center = total / width
    square = 0.0
    for ref in pieces:
        square = square + jnp.sum((ref[...].astype(jnp.float32) - center) ** 2, axis=0, keepdims=True)
    scale = lax.rsqrt(square / width + 1e-05)
    for ref, spot in zip(pieces, spots):
        rows = pl.ds(pl.multiple_of(spot, 64), ref.shape[0])
        value = (ref[...].astype(jnp.float32) - center) * scale * gain_ref[rows, :]
        out_ref[rows, :] = value.astype(jnp.bfloat16)


def first_kernel(offset, held, coming, layout, info_ref, bias_ref, w_ref, *refs):
    tile = 256
    buf, sems = refs[-2:]
    refs = refs[:-2]
    if coming is not None:
        next_buf, refs = refs[-1], refs[:-1]
    out_ref, refs = refs[-1], refs[:-1]
    if held:
        block_ref, refs = refs[0], refs[1:]
    steps = out_ref.shape[0] // tile
    streamed = steps - held

    def copy(step):
        start = pl.multiple_of(offset + step * tile, tile)
        return pltpu.make_async_copy(w_ref.at[0, pl.ds(start, tile), :], buf.at[step - held], sems.at[step - held])

    def copy_next():
        return pltpu.make_async_copy(w_ref.at[0, pl.ds(coming, next_buf.shape[0]), :], next_buf, sems.at[streamed])

    for step in range(held, steps):
        copy(step).start()
    if coming is not None:
        copy_next().start()
    if layout is None:
        normed_ref = refs[0]
    else:
        gain_ref, pieces, normed_ref = refs[0], refs[1:-1], refs[-1]
        part, half, places = layout
        seg = info_ref[0]
        spots = [info_ref[1 + k] * part + row + seg * half for k, row in places]
        spots += [info_ref[1 + k] * part + row + (1 - seg) * half for k, row in places]
        normalize(pieces, spots, gain_ref, normed_ref)

    def finish(step, weights):
        at = pl.multiple_of(step * tile, tile)
        pre = jnp.dot(weights, normed_ref[...], preferred_element_type=jnp.float32)
        pre = pre + bias_ref[pl.ds(pl.multiple_of(offset + at, tile), tile), :]
        out_ref[pl.ds(at, tile), :] = jax.nn.gelu(pre, approximate=True).astype(jnp.bfloat16)

    def at_hand(step, carry):
        finish(step, block_ref[pl.ds(pl.multiple_of(step * tile, tile), tile), :])
        return carry

    def stream(step, carry):
        copy(step).wait()
        finish(step, buf[step - held])
        return carry

    if held:
        lax.fori_loop(0, held, at_hand, 0)
    lax.fori_loop(held, steps, stream, 0)
    if coming is not None:
        copy_next().wait()


def first_matmul(info, bias, w, offset, rows, block=None, coming=None, ahead=0, normed=None, gain=None, pieces=(), layout=None):
    tile = 256
    width, tokens = w.shape[2], bias.shape[1]
    held = 0 if block is None else block.shape[0] // tile
    streamed = rows // tile - held
    outs = [jax.ShapeDtypeStruct((rows, tokens), jnp.bfloat16)]
    if layout is None:
        args = [normed]
    else:
        args = [gain, *pieces]
        outs = [jax.ShapeDtypeStruct((width, tokens), jnp.bfloat16)] + outs
    if block is not None:
        args = [block, *args]
    if coming is not None:
        outs.append(jax.ShapeDtypeStruct((ahead, width), jnp.bfloat16))
    call = pallas(
        functools.partial(first_kernel, offset, held, coming, layout),
        outs,
        [SM, VM, ANY] + [VM] * len(args),
        [VM] * len(outs),
        [pltpu.VMEM((streamed, tile, width), jnp.bfloat16), pltpu.SemaphoreType.DMA((streamed + 1,))],
        flops=2 * rows * width * tokens,
        moved=2 * rows * width,
    )
    results = call(info, bias, w, *args)
    return results if len(outs) > 1 else results[0]


def pick_kernel(phase, info_ref, here_ref, crossed_ref, *outs):
    rows = outs[0].shape[0]

    @pl.when(info_ref[0] == phase)
    def _():
        for number, out_ref in enumerate(outs):
            out_ref[...] = here_ref[pl.ds(number * rows, rows), :]

    @pl.when(info_ref[0] != phase)
    def _():
        for number, out_ref in enumerate(outs):
            out_ref[...] = crossed_ref[pl.ds(number * rows, rows), :]


def pick(phase, info, here, crossed, count):
    out = jax.ShapeDtypeStruct((here.shape[0] // count, here.shape[1]), here.dtype)
    kernel = functools.partial(pick_kernel, phase)
    return pallas(kernel, [out] * count, [SM, VM, VM], [VM] * count, limit=8)(info, here, crossed)


def relay_kernel(info_ref, kept_ref, swapped_ref, out_ref, own_ref):
    half = own_ref.shape[0]

    @pl.when(info_ref[0] == 0)
    def _():
        out_ref[...] = kept_ref[...]
        own_ref[...] = kept_ref[:half]

    @pl.when(info_ref[0] != 0)
    def _():
        out_ref[...] = swapped_ref[...]
        own_ref[...] = swapped_ref[half:]


def relay(info, kept, swapped):
    half = (kept.shape[0] // 2, kept.shape[1])
    outs = [jax.ShapeDtypeStruct(kept.shape, kept.dtype), jax.ShapeDtypeStruct(half, kept.dtype)]
    return pallas(relay_kernel, outs, [SM, VM, VM], [VM, VM], limit=8)(info, kept, swapped)


def halve_kernel(front_ref, back_ref, lower_ref, upper_ref):
    mid = lower_ref.shape[0]
    lower_ref[...] = front_ref[:mid]
    upper_ref[...] = back_ref[mid:]


def halve(front, back):
    mid = front.shape[0] // 2
    outs = [
        jax.ShapeDtypeStruct((mid, front.shape[1]), front.dtype),
        jax.ShapeDtypeStruct((front.shape[0] - mid, front.shape[1]), front.dtype),
    ]
    return pallas(halve_kernel, outs, [VM, VM], [VM, VM], limit=8)(front, back)


def column_copies(info_ref, w_ref, buf, sems, places, t, tile):
    down = pl.ds(pl.multiple_of(t * tile, tile), tile)
    at = 0
    for i, (k, scale, row, rows) in enumerate(places):
        columns = pl.ds(pl.multiple_of(info_ref[1 + k] * scale + row, 128), rows)
        yield pltpu.make_async_copy(w_ref.at[0, down, columns], buf.at[down, pl.ds(at, rows)], sems.at[t, i])
        at += rows


def second_kernel(places, coming, held, first, ending, *refs):
    count = len(places)
    info_ref, w_ref = refs[:2]
    pieces, refs = refs[2 : 2 + count], refs[2 + count :]
    if held is not None:
        buf, refs = refs[0], refs[1:]
    if not first:
        acc_ref, refs = refs[0], refs[1:]
    if coming:
        next_sems, refs = refs[-1], refs[:-1]
    if held is None:
        buf, sems, refs = refs[-2], refs[-1], refs[:-2]
    joined, refs = refs[-1], refs[:-1]
    if coming:
        next_buf, refs = refs[-1], refs[:-1]
    depth, tile = w_ref.shape[1], 256
    tiles = depth // tile

    def start(t, carry):
        for copy in column_copies(info_ref, w_ref, buf, sems, places, t, tile):
            copy.start()
        return carry

    def start_next(t, carry):
        for copy in column_copies(info_ref, w_ref, next_buf, next_sems, coming, t, tile):
            copy.start()
        return carry

    def wait_next(t, carry):
        for copy in column_copies(info_ref, w_ref, next_buf, next_sems, coming, t, tile):
            copy.wait()
        return carry

    if held is None:
        lax.fori_loop(0, tiles, start, 0)
    if coming:
        lax.fori_loop(0, tiles, start_next, 0)
    at = 0
    for ref in pieces:
        joined[pl.ds(at, ref.shape[0]), :] = ref[...]
        at += ref.shape[0]
    span = pl.ds(0 if held is None else held, at)

    def body(t, carry):
        if held is None:
            for copy in column_copies(info_ref, w_ref, buf, sems, places, t, tile):
                copy.wait()
        own = pl.ds(pl.multiple_of(t * tile, tile), tile)
        acc = jnp.dot(buf[own, span], joined[...], preferred_element_type=jnp.float32)
        if not first:
            acc = acc_ref[own, :] + acc
        if not ending:
            refs[0][own, :] = acc
            return carry
        local_ref, bias_ref = refs[:2]
        result = local_ref[own, :].astype(jnp.float32) + (acc + bias_ref[own, :])
        if ending == 1:
            refs[2][own, :] = result.astype(jnp.bfloat16)
        else:
            early_ref, out_ref = refs[2:]
            rounded = result.astype(jnp.bfloat16).astype(jnp.float32)
            result = jnp.where(info_ref[0] == 0, early_ref[own, :].astype(jnp.float32), rounded)
            out_ref[:, own] = result.T.astype(jnp.bfloat16)
        return carry

    lax.fori_loop(0, tiles, body, 0)
    if coming:
        lax.fori_loop(0, tiles, wait_next, 0)


def second_matmul(info, acc, pieces, places, w, coming=(), buf=None, held=None, ends=()):
    depth, tokens = w.shape[1], pieces[0].shape[1]
    total = sum(piece.shape[0] for piece in pieces)
    ahead = sum(rows for *_, rows in coming)
    ending = max(0, len(ends) - 1)
    args = [info, w, *pieces]
    args += ([] if buf is None else [buf]) + ([] if acc is None else [acc]) + list(ends)
    if ending == 2:
        out = jax.ShapeDtypeStruct((tokens, depth), jnp.bfloat16)
    else:
        out = jax.ShapeDtypeStruct((depth, tokens), jnp.bfloat16 if ending else jnp.float32)
    outs, out_specs = [out], [VM]
    scratch = [pltpu.VMEM((total, tokens), jnp.bfloat16)]
    if buf is None:
        scratch += [
            pltpu.VMEM((depth, total), jnp.bfloat16),
            pltpu.SemaphoreType.DMA((depth // 256, len(pieces))),
        ]
    if coming:
        outs.append(jax.ShapeDtypeStruct((depth, ahead), jnp.bfloat16))
        out_specs.append(VM)
        scratch.append(pltpu.SemaphoreType.DMA((depth // 256, len(coming))))
    kernel = functools.partial(second_kernel, places, coming, held, acc is None, ending)
    cost = dict(flops=2 * depth * total * tokens, moved=2 * depth * total)
    call = pallas(kernel, outs, [SM, ANY] + [VM] * (len(args) - 2), out_specs, scratch, **cost)
    results = call(*args)
    return results if coming else results[0]


def ring_shards(ring, inputs, norm_gain, w_in, b_in, w_out, b_out):
    n = len(ring)
    last = n // 2
    tokens, part = inputs.shape[1:]
    half = part // 2
    width = norm_gain.shape[1]
    hidden = w_in.shape[1]
    side = hidden // 2
    seg = lax.axis_index("segment")
    place = {device: at for at, device in enumerate(ring)}
    behind = np.array([[ring[(place[t] - k) % n] for k in range(n)] for t in range(n)], np.int32)
    owner = jnp.asarray(behind)[lax.axis_index("tp")]
    info = jnp.concatenate([seg.reshape(1).astype(jnp.int32), owner])

    def hop(value, steps):
        return lax.ppermute(value, "tp", [(ring[at], ring[(at + steps) % n]) for at in range(n)])

    def swap(value):
        return lax.ppermute(value, "segment", [(0, 1), (1, 0)])

    def over_lanes(row):
        return jnp.broadcast_to(row[0][:, None], (row.shape[1], tokens))

    local = inputs[0].T
    own = lax.dynamic_slice_in_dim(inputs[0], seg * half, half, 1).T
    mid = half // 2
    x_places = [(0, 0)] + [(k, 0) for step in range(1, last) for k in (step, n - step)] + [(last, 0), (last, mid)]

    early = None
    for phase in range(2):
        front = back = own
        mine, theirs = [own], [swap(own)]
        for step in range(1, last + 1):
            if step == last:
                front, back = halve(front, back)
            ready = front
            front, back = hop(front, 1), hop(back, -1)
            if phase == 0 and step == 1:
                front, back, info, local = lax.optimization_barrier((front, back, info, local))
            if phase == 0 and step == 2:
                _, gain = lax.optimization_barrier((ready, norm_gain))
                front, back, gain = lax.optimization_barrier((front, back, over_lanes(gain)))
            if phase == 0 and step == 3:
                _, bias_in, bias_out = lax.optimization_barrier((ready, b_in, b_out))
                front, back, bias_in, bias_out = lax.optimization_barrier(
                    (front, back, over_lanes(bias_in), over_lanes(bias_out))
                )
            mine += [front, back]
            theirs += [swap(front), swap(back)]
        ahead = side // 3
        layout = (part, half, x_places)
        normed, other, block = first_matmul(
            info, bias_in, w_in, side, side, coming=0, ahead=ahead, gain=gain, pieces=mine + theirs, layout=layout
        )
        crossed = swap(other)
        here = first_matmul(info, bias_in, w_in, 0, side, block=block, normed=normed)
        fronts = pick(phase, info, here, crossed, CHUNKS)
        backs = list(fronts)
        fronts = list(fronts)
        chunk = side // CHUNKS
        plans = [[(0, hidden, 0, side), (0, hidden, side, side)]]
        for step in range(1, last + 1):
            rows, at = (chunk // 2, chunk // 2) if step == last else (chunk, 0)
            plan = []
            for c in range(CHUNKS):
                plan += [(step, hidden, c * chunk, rows), (n - step, hidden, c * chunk + at, rows)]
            plans.append(plan + [(k, hidden, row + side, rows) for k, _, row, _ in plan])
        acc = buf = held = None
        pieces = [here, other]
        for step in range(1, last + 1):
            for c in range(CHUNKS):
                if step == last:
                    fronts[c], backs[c] = halve(fronts[c], backs[c])
                fronts[c], backs[c] = hop(fronts[c], 1), hop(backs[c], -1)
            acc, buf = second_matmul(info, acc, pieces, plans[step - 1], w_out, plans[step], buf, held)
            held = 0
            for c in range(CHUNKS):
                fronts[c], backs[c], _ = lax.optimization_barrier((fronts[c], backs[c], acc))
            pieces = [piece for pair in zip(fronts, backs) for piece in pair]
            pieces += [swap(piece) for piece in pieces]
        count = len(pieces) // 2
        acc = second_matmul(info, acc, pieces[:count], plans[last][:count], w_out, buf=buf, held=0)
        ends = [local, bias_out] + ([] if early is None else [early])
        result = second_matmul(info, acc, pieces[count:], plans[last][count:], w_out, buf=buf, held=side, ends=ends)
        if phase == 0:
            early = result
            local, own = relay(info, early, swap(early))
    return result.reshape(1, 1, tokens, part)


def snake(mesh):
    n = mesh.shape["tp"]
    return [2 * at for at in range(n // 2)] + [2 * at + 1 for at in reversed(range(n // 2))]


def solution(mesh):
    def shards(inputs, norm_gain, w_in, b_in, w_out, b_out):
        small = mesh.shape["tp"] == 8 and mesh.shape["segment"] == 2 and inputs.shape[0] == 1
        if small and inputs.shape[2] % 512 == 0 or small and inputs.shape[2] % 768 == 0:
            return ring_shards(snake(mesh), inputs, norm_gain, w_in, b_in, w_out, b_out)
        return plain_shards(inputs, norm_gain, w_in, b_in, w_out, b_out)

    return jax.shard_map(
        shards,
        mesh=mesh,
        in_specs=(
            P(None, "dp", "tp"),
            P("segment", None),
            P("segment", "tp", None),
            P("segment", "tp"),
            P("segment", "tp", None),
            P("segment", "tp"),
        ),
        out_specs=P("segment", None, "dp", "tp"),
        check_vma=False,
    )
```

```python
import functools

import jax
import jax.numpy as jnp
import numpy as np
from jax import lax
from jax.experimental import pallas as pl
from jax.experimental.pallas import tpu as pltpu
from jax.sharding import PartitionSpec as P

MIB = 1024 * 1024
VM = pl.BlockSpec(memory_space=pltpu.VMEM)
SM = pl.BlockSpec(memory_space=pltpu.SMEM)
ANY = pl.BlockSpec(memory_space=pl.ANY)
CHUNKS = 1


def shifted(value, axis, steps):
    count = lax.axis_size(axis)
    first, last = (max(0, -steps), min(count, count - steps))
    return lax.ppermute(value, axis, [(source, source + steps) for source in range(first, last)])


def contract(left, right):
    return lax.dot_general(
        left, right, (((1,), (1,)), ((), ())), preferred_element_type=jnp.float32
    )


def plain_section(local, gain, w_first, b_first, w_second, b_second):
    whole = lax.all_gather(local, "tp", axis=1, tiled=True)
    values = whole.astype(jnp.float32)
    center = jnp.mean(values, axis=1, keepdims=True)
    spread = jnp.mean((values - center) ** 2, axis=1, keepdims=True)
    normed = ((values - center) * lax.rsqrt(spread + 1e-05) * gain).astype(jnp.bfloat16)
    pre = contract(normed, w_first) + b_first
    hidden = jax.nn.gelu(pre, approximate=True).astype(jnp.bfloat16)
    branch = contract(lax.all_gather(hidden, "tp", axis=1, tiled=True), w_second)
    return (local.astype(jnp.float32) + branch + b_second).astype(jnp.bfloat16)


def plain_shards(inputs, norm_gain, w_in, b_in, w_out, b_out):
    batches, tok_rows, width = inputs.shape
    first_segment = lax.axis_index("segment") == 0
    incoming = jnp.zeros((tok_rows, width), jnp.bfloat16)
    results = []
    for tick in range(batches + 1):
        own = inputs[min(tick, batches - 1)]
        current = jnp.where(first_segment, own, incoming)
        result = plain_section(current, norm_gain[0], w_in[0], b_in[0], w_out[0], b_out[0])
        results.append(result)
        if tick < batches:
            incoming = shifted(result, "segment", 1)
    early = jnp.stack(results[:batches])
    late = jnp.stack(results[1:])
    chosen = jnp.where(first_segment, early, late)
    return chosen.reshape(1, batches, tok_rows, width)


def pallas(kernel, outs, specs, out_specs, scratch=(), limit=28, flops=0, moved=0):
    return pl.pallas_call(
        kernel,
        out_shape=outs,
        in_specs=specs,
        out_specs=out_specs,
        scratch_shapes=list(scratch),
        compiler_params=pltpu.CompilerParams(vmem_limit_bytes=limit * MIB),
        cost_estimate=pl.CostEstimate(flops=flops, bytes_accessed=moved, transcendentals=0),
    )


def normalize(pieces, spots, gain_ref, out_ref):
    width = out_ref.shape[0]
    total = 0.0
    for ref in pieces:
        total = total + jnp.sum(ref[...].astype(jnp.float32), axis=0, keepdims=True)
    center = total / width
    square = 0.0
    for ref in pieces:
        square = square + jnp.sum((ref[...].astype(jnp.float32) - center) ** 2, axis=0, keepdims=True)
    scale = lax.rsqrt(square / width + 1e-05)
    for ref, spot in zip(pieces, spots):
        rows = pl.ds(pl.multiple_of(spot, 64), ref.shape[0])
        value = (ref[...].astype(jnp.float32) - center) * scale * gain_ref[rows, :]
        out_ref[rows, :] = value.astype(jnp.bfloat16)


def first_kernel(offset, held, coming, layout, info_ref, bias_ref, w_ref, *refs):
    tile = 256
    buf, sems = refs[-2:]
    refs = refs[:-2]
    if coming is not None:
        next_buf, refs = refs[-1], refs[:-1]
    out_ref, refs = refs[-1], refs[:-1]
    if held:
        block_ref, refs = refs[0], refs[1:]
    steps = out_ref.shape[0] // tile
    streamed = steps - held

    def copy(step):
        start = pl.multiple_of(offset + step * tile, tile)
        return pltpu.make_async_copy(w_ref.at[0, pl.ds(start, tile), :], buf.at[step - held], sems.at[step - held])

    def copy_next():
        return pltpu.make_async_copy(w_ref.at[0, pl.ds(coming, next_buf.shape[0]), :], next_buf, sems.at[streamed])

    for step in range(held, steps):
        copy(step).start()
    if coming is not None:
        copy_next().start()
    if layout is None:
        normed_ref = refs[0]
    else:
        gain_ref, pieces, normed_ref = refs[0], refs[1:-1], refs[-1]
        part, half, places = layout
        seg = info_ref[0]
        spots = [info_ref[1 + k] * part + row + seg * half for k, row in places]
        spots += [info_ref[1 + k] * part + row + (1 - seg) * half for k, row in places]
        normalize(pieces, spots, gain_ref, normed_ref)

    def finish(step, weights):
        at = pl.multiple_of(step * tile, tile)
        pre = jnp.dot(weights, normed_ref[...], preferred_element_type=jnp.float32)
        pre = pre + bias_ref[pl.ds(pl.multiple_of(offset + at, tile), tile), :]
        out_ref[pl.ds(at, tile), :] = jax.nn.gelu(pre, approximate=True).astype(jnp.bfloat16)

    def at_hand(step, carry):
        finish(step, block_ref[pl.ds(pl.multiple_of(step * tile, tile), tile), :])
        return carry

    def stream(step, carry):
        copy(step).wait()
        finish(step, buf[step - held])
        return carry

    if held:
        lax.fori_loop(0, held, at_hand, 0)
    lax.fori_loop(held, steps, stream, 0)
    if coming is not None:
        copy_next().wait()


def first_matmul(info, bias, w, offset, rows, block=None, coming=None, ahead=0, normed=None, gain=None, pieces=(), layout=None):
    tile = 256
    width, tokens = w.shape[2], bias.shape[1]
    held = 0 if block is None else block.shape[0] // tile
    streamed = rows // tile - held
    outs = [jax.ShapeDtypeStruct((rows, tokens), jnp.bfloat16)]
    if layout is None:
        args = [normed]
    else:
        args = [gain, *pieces]
        outs = [jax.ShapeDtypeStruct((width, tokens), jnp.bfloat16)] + outs
    if block is not None:
        args = [block, *args]
    if coming is not None:
        outs.append(jax.ShapeDtypeStruct((ahead, width), jnp.bfloat16))
    call = pallas(
        functools.partial(first_kernel, offset, held, coming, layout),
        outs,
        [SM, VM, ANY] + [VM] * len(args),
        [VM] * len(outs),
        [pltpu.VMEM((streamed, tile, width), jnp.bfloat16), pltpu.SemaphoreType.DMA((streamed + 1,))],
        flops=2 * rows * width * tokens,
        moved=2 * rows * width,
    )
    results = call(info, bias, w, *args)
    return results if len(outs) > 1 else results[0]


def pick_kernel(phase, info_ref, here_ref, crossed_ref, *outs):
    rows = outs[0].shape[0]

    @pl.when(info_ref[0] == phase)
    def _():
        for number, out_ref in enumerate(outs):
            out_ref[...] = here_ref[pl.ds(number * rows, rows), :]

    @pl.when(info_ref[0] != phase)
    def _():
        for number, out_ref in enumerate(outs):
            out_ref[...] = crossed_ref[pl.ds(number * rows, rows), :]


def pick(phase, info, here, crossed, count):
    out = jax.ShapeDtypeStruct((here.shape[0] // count, here.shape[1]), here.dtype)
    kernel = functools.partial(pick_kernel, phase)
    return pallas(kernel, [out] * count, [SM, VM, VM], [VM] * count, limit=8)(info, here, crossed)


def relay_kernel(info_ref, kept_ref, swapped_ref, out_ref, own_ref):
    half = own_ref.shape[0]

    @pl.when(info_ref[0] == 0)
    def _():
        out_ref[...] = kept_ref[...]
        own_ref[...] = kept_ref[:half]

    @pl.when(info_ref[0] != 0)
    def _():
        out_ref[...] = swapped_ref[...]
        own_ref[...] = swapped_ref[half:]


def relay(info, kept, swapped):
    half = (kept.shape[0] // 2, kept.shape[1])
    outs = [jax.ShapeDtypeStruct(kept.shape, kept.dtype), jax.ShapeDtypeStruct(half, kept.dtype)]
    return pallas(relay_kernel, outs, [SM, VM, VM], [VM, VM], limit=8)(info, kept, swapped)


def halve_kernel(front_ref, back_ref, lower_ref, upper_ref):
    mid = lower_ref.shape[0]
    lower_ref[...] = front_ref[:mid]
    upper_ref[...] = back_ref[mid:]


def halve(front, back):
    mid = front.shape[0] // 2
    outs = [
        jax.ShapeDtypeStruct((mid, front.shape[1]), front.dtype),
        jax.ShapeDtypeStruct((front.shape[0] - mid, front.shape[1]), front.dtype),
    ]
    return pallas(halve_kernel, outs, [VM, VM], [VM, VM], limit=8)(front, back)


def column_copies(info_ref, w_ref, buf, sems, places, t, tile):
    down = pl.ds(pl.multiple_of(t * tile, tile), tile)
    at = 0
    for i, (k, scale, row, rows) in enumerate(places):
        columns = pl.ds(pl.multiple_of(info_ref[1 + k] * scale + row, 128), rows)
        yield pltpu.make_async_copy(w_ref.at[0, down, columns], buf.at[down, pl.ds(at, rows)], sems.at[t, i])
        at += rows


def second_kernel(places, coming, held, first, ending, *refs):
    count = len(places)
    info_ref, w_ref = refs[:2]
    pieces, refs = refs[2 : 2 + count], refs[2 + count :]
    if held is not None:
        buf, refs = refs[0], refs[1:]
    if not first:
        acc_ref, refs = refs[0], refs[1:]
    if coming:
        next_sems, refs = refs[-1], refs[:-1]
    if held is None:
        buf, sems, refs = refs[-2], refs[-1], refs[:-2]
    joined, refs = refs[-1], refs[:-1]
    if coming:
        next_buf, refs = refs[-1], refs[:-1]
    depth, tile = w_ref.shape[1], 256
    tiles = depth // tile

    def start(t, carry):
        for copy in column_copies(info_ref, w_ref, buf, sems, places, t, tile):
            copy.start()
        return carry

    def start_next(t, carry):
        for copy in column_copies(info_ref, w_ref, next_buf, next_sems, coming, t, tile):
            copy.start()
        return carry

    def wait_next(t, carry):
        for copy in column_copies(info_ref, w_ref, next_buf, next_sems, coming, t, tile):
            copy.wait()
        return carry

    if held is None:
        lax.fori_loop(0, tiles, start, 0)
    if coming:
        lax.fori_loop(0, tiles, start_next, 0)
    at = 0
    for ref in pieces:
        joined[pl.ds(at, ref.shape[0]), :] = ref[...]
        at += ref.shape[0]
    span = pl.ds(0 if held is None else held, at)

    def body(t, carry):
        if held is None:
            for copy in column_copies(info_ref, w_ref, buf, sems, places, t, tile):
                copy.wait()
        own = pl.ds(pl.multiple_of(t * tile, tile), tile)
        acc = jnp.dot(buf[own, span], joined[...], preferred_element_type=jnp.float32)
        if not first:
            acc = acc_ref[own, :] + acc
        if not ending:
            refs[0][own, :] = acc
            return carry
        local_ref, bias_ref = refs[:2]
        result = local_ref[own, :].astype(jnp.float32) + (acc + bias_ref[own, :])
        if ending == 1:
            refs[2][own, :] = result.astype(jnp.bfloat16)
        else:
            early_ref, out_ref = refs[2:]
            rounded = result.astype(jnp.bfloat16).astype(jnp.float32)
            result = jnp.where(info_ref[0] == 0, early_ref[own, :].astype(jnp.float32), rounded)
            out_ref[:, own] = result.T.astype(jnp.bfloat16)
        return carry

    lax.fori_loop(0, tiles, body, 0)
    if coming:
        lax.fori_loop(0, tiles, wait_next, 0)


def second_matmul(info, acc, pieces, places, w, coming=(), buf=None, held=None, ends=()):
    depth, tokens = w.shape[1], pieces[0].shape[1]
    total = sum(piece.shape[0] for piece in pieces)
    ahead = sum(rows for *_, rows in coming)
    ending = max(0, len(ends) - 1)
    args = [info, w, *pieces]
    args += ([] if buf is None else [buf]) + ([] if acc is None else [acc]) + list(ends)
    if ending == 2:
        out = jax.ShapeDtypeStruct((tokens, depth), jnp.bfloat16)
    else:
        out = jax.ShapeDtypeStruct((depth, tokens), jnp.bfloat16 if ending else jnp.float32)
    outs, out_specs = [out], [VM]
    scratch = [pltpu.VMEM((total, tokens), jnp.bfloat16)]
    if buf is None:
        scratch += [
            pltpu.VMEM((depth, total), jnp.bfloat16),
            pltpu.SemaphoreType.DMA((depth // 256, len(pieces))),
        ]
    if coming:
        outs.append(jax.ShapeDtypeStruct((depth, ahead), jnp.bfloat16))
        out_specs.append(VM)
        scratch.append(pltpu.SemaphoreType.DMA((depth // 256, len(coming))))
    kernel = functools.partial(second_kernel, places, coming, held, acc is None, ending)
    cost = dict(flops=2 * depth * total * tokens, moved=2 * depth * total)
    call = pallas(kernel, outs, [SM, ANY] + [VM] * (len(args) - 2), out_specs, scratch, **cost)
    results = call(*args)
    return results if coming else results[0]


def ring_shards(ring, inputs, norm_gain, w_in, b_in, w_out, b_out):
    n = len(ring)
    last = n // 2
    tokens, part = inputs.shape[1:]
    half = part // 2
    width = norm_gain.shape[1]
    hidden = w_in.shape[1]
    side = hidden // 2
    seg = lax.axis_index("segment")
    place = {device: at for at, device in enumerate(ring)}
    behind = np.array([[ring[(place[t] - k) % n] for k in range(n)] for t in range(n)], np.int32)
    owner = jnp.asarray(behind)[lax.axis_index("tp")]
    info = jnp.concatenate([seg.reshape(1).astype(jnp.int32), owner])

    def hop(value, steps):
        return lax.ppermute(value, "tp", [(ring[at], ring[(at + steps) % n]) for at in range(n)])

    def swap(value):
        return lax.ppermute(value, "segment", [(0, 1), (1, 0)])

    def over_lanes(row):
        return jnp.broadcast_to(row[0][:, None], (row.shape[1], tokens))

    local = inputs[0].T
    own = lax.dynamic_slice_in_dim(inputs[0], seg * half, half, 1).T
    x_places = [(0, 0)] + [(k, 0) for step in range(1, last) for k in (step, n - step)] + [(last, 0)]

    early = None
    for phase in range(2):
        front = back = own
        mine, theirs = [own], [swap(own)]
        for step in range(1, last + 1):
            ready = front
            front, back = hop(front, 1), hop(back, -1) if step < last else None
            if phase == 0 and step == 1:
                front, back, info, local = lax.optimization_barrier((front, back, info, local))
            if phase == 0 and step == 2:
                _, gain = lax.optimization_barrier((ready, norm_gain))
                front, back, gain = lax.optimization_barrier((front, back, over_lanes(gain)))
            if phase == 0 and step == 3:
                _, bias_in, bias_out = lax.optimization_barrier((ready, b_in, b_out))
                front, back, bias_in, bias_out = lax.optimization_barrier(
                    (front, back, over_lanes(bias_in), over_lanes(bias_out))
                )
            mine += [front] if step == last else [front, back]
            theirs += [swap(front)] if step == last else [swap(front), swap(back)]
        ahead = side // 3
        layout = (part, half, x_places)
        normed, other, block = first_matmul(
            info, bias_in, w_in, side, side, coming=0, ahead=ahead, gain=gain, pieces=mine + theirs, layout=layout
        )
        crossed = swap(other)
        here = first_matmul(info, bias_in, w_in, 0, side, block=block, normed=normed)
        fronts = pick(phase, info, here, crossed, CHUNKS)
        backs = list(fronts)
        fronts = list(fronts)
        chunk = side // CHUNKS
        plans = [[(0, hidden, 0, side), (0, hidden, side, side)]]
        for step in range(1, last + 1):
            rows, at = (chunk // 2, chunk // 2) if step == last else (chunk, 0)
            plan = []
            for c in range(CHUNKS):
                plan += [(step, hidden, c * chunk, rows), (n - step, hidden, c * chunk + at, rows)]
            plans.append(plan + [(k, hidden, row + side, rows) for k, _, row, _ in plan])
        acc = buf = held = None
        pieces = [here, other]
        for step in range(1, last + 1):
            for c in range(CHUNKS):
                if step == last:
                    fronts[c], backs[c] = halve(fronts[c], backs[c])
                fronts[c], backs[c] = hop(fronts[c], 1), hop(backs[c], -1)
            acc, buf = second_matmul(info, acc, pieces, plans[step - 1], w_out, plans[step], buf, held)
            held = 0
            for c in range(CHUNKS):
                fronts[c], backs[c], _ = lax.optimization_barrier((fronts[c], backs[c], acc))
            pieces = [piece for pair in zip(fronts, backs) for piece in pair]
            pieces += [swap(piece) for piece in pieces]
        count = len(pieces) // 2
        acc = second_matmul(info, acc, pieces[:count], plans[last][:count], w_out, buf=buf, held=0)
        ends = [local, bias_out] + ([] if early is None else [early])
        result = second_matmul(info, acc, pieces[count:], plans[last][count:], w_out, buf=buf, held=side, ends=ends)
        if phase == 0:
            early = result
            local, own = relay(info, early, swap(early))
    return result.reshape(1, 1, tokens, part)


def snake(mesh):
    n = mesh.shape["tp"]
    return [2 * at for at in range(n // 2)] + [2 * at + 1 for at in reversed(range(n // 2))]


def solution(mesh):
    def shards(inputs, norm_gain, w_in, b_in, w_out, b_out):
        small = mesh.shape["tp"] == 8 and mesh.shape["segment"] == 2 and inputs.shape[0] == 1
        if small and inputs.shape[2] % 512 == 0 or small and inputs.shape[2] % 768 == 0:
            return ring_shards(snake(mesh), inputs, norm_gain, w_in, b_in, w_out, b_out)
        return plain_shards(inputs, norm_gain, w_in, b_in, w_out, b_out)

    return jax.shard_map(
        shards,
        mesh=mesh,
        in_specs=(
            P(None, "dp", "tp"),
            P("segment", None),
            P("segment", "tp", None),
            P("segment", "tp"),
            P("segment", "tp", None),
            P("segment", "tp"),
        ),
        out_specs=P("segment", None, "dp", "tp"),
        check_vma=False,
    )
```

```python
import functools

import jax
import jax.numpy as jnp
import numpy as np
from jax import lax
from jax.experimental import pallas as pl
from jax.experimental.pallas import tpu as pltpu
from jax.sharding import PartitionSpec as P

MIB = 1024 * 1024
VM = pl.BlockSpec(memory_space=pltpu.VMEM)
SM = pl.BlockSpec(memory_space=pltpu.SMEM)
ANY = pl.BlockSpec(memory_space=pl.ANY)
CHUNKS = 1


def shifted(value, axis, steps):
    count = lax.axis_size(axis)
    first, last = (max(0, -steps), min(count, count - steps))
    return lax.ppermute(value, axis, [(source, source + steps) for source in range(first, last)])


def contract(left, right):
    return lax.dot_general(
        left, right, (((1,), (1,)), ((), ())), preferred_element_type=jnp.float32
    )


def plain_section(local, gain, w_first, b_first, w_second, b_second):
    whole = lax.all_gather(local, "tp", axis=1, tiled=True)
    values = whole.astype(jnp.float32)
    center = jnp.mean(values, axis=1, keepdims=True)
    spread = jnp.mean((values - center) ** 2, axis=1, keepdims=True)
    normed = ((values - center) * lax.rsqrt(spread + 1e-05) * gain).astype(jnp.bfloat16)
    pre = contract(normed, w_first) + b_first
    hidden = jax.nn.gelu(pre, approximate=True).astype(jnp.bfloat16)
    branch = contract(lax.all_gather(hidden, "tp", axis=1, tiled=True), w_second)
    return (local.astype(jnp.float32) + branch + b_second).astype(jnp.bfloat16)


def plain_shards(inputs, norm_gain, w_in, b_in, w_out, b_out):
    batches, tok_rows, width = inputs.shape
    first_segment = lax.axis_index("segment") == 0
    incoming = jnp.zeros((tok_rows, width), jnp.bfloat16)
    results = []
    for tick in range(batches + 1):
        own = inputs[min(tick, batches - 1)]
        current = jnp.where(first_segment, own, incoming)
        result = plain_section(current, norm_gain[0], w_in[0], b_in[0], w_out[0], b_out[0])
        results.append(result)
        if tick < batches:
            incoming = shifted(result, "segment", 1)
    early = jnp.stack(results[:batches])
    late = jnp.stack(results[1:])
    chosen = jnp.where(first_segment, early, late)
    return chosen.reshape(1, batches, tok_rows, width)


def pallas(kernel, outs, specs, out_specs, scratch=(), limit=28, flops=0, moved=0):
    return pl.pallas_call(
        kernel,
        out_shape=outs,
        in_specs=specs,
        out_specs=out_specs,
        scratch_shapes=list(scratch),
        compiler_params=pltpu.CompilerParams(vmem_limit_bytes=limit * MIB),
        cost_estimate=pl.CostEstimate(flops=flops, bytes_accessed=moved, transcendentals=0),
    )


def normalize(pieces, spots, gain_ref, out_ref):
    width = out_ref.shape[0]
    total = 0.0
    for ref in pieces:
        total = total + jnp.sum(ref[...].astype(jnp.float32), axis=0, keepdims=True)
    center = total / width
    square = 0.0
    for ref in pieces:
        square = square + jnp.sum((ref[...].astype(jnp.float32) - center) ** 2, axis=0, keepdims=True)
    scale = lax.rsqrt(square / width + 1e-05)
    for ref, spot in zip(pieces, spots):
        rows = pl.ds(pl.multiple_of(spot, 64), ref.shape[0])
        value = (ref[...].astype(jnp.float32) - center) * scale * gain_ref[rows, :]
        out_ref[rows, :] = value.astype(jnp.bfloat16)


def first_kernel(offset, held, coming, layout, info_ref, bias_ref, w_ref, *refs):
    tile = 256
    buf, sems = refs[-2:]
    refs = refs[:-2]
    if coming is not None:
        next_buf, refs = refs[-1], refs[:-1]
    out_ref, refs = refs[-1], refs[:-1]
    if held:
        block_ref, refs = refs[0], refs[1:]
    steps = out_ref.shape[0] // tile
    streamed = steps - held

    def copy(step):
        start = pl.multiple_of(offset + step * tile, tile)
        return pltpu.make_async_copy(w_ref.at[0, pl.ds(start, tile), :], buf.at[step - held], sems.at[step - held])

    def copy_next():
        return pltpu.make_async_copy(w_ref.at[0, pl.ds(coming, next_buf.shape[0]), :], next_buf, sems.at[streamed])

    for step in range(held, steps):
        copy(step).start()
    if coming is not None:
        copy_next().start()
    if layout is None:
        normed_ref = refs[0]
    else:
        gain_ref, pieces, normed_ref = refs[0], refs[1:-1], refs[-1]
        part, half, places = layout
        seg = info_ref[0]
        spots = [info_ref[1 + k] * part + row + seg * half for k, row in places]
        spots += [info_ref[1 + k] * part + row + (1 - seg) * half for k, row in places]
        normalize(pieces, spots, gain_ref, normed_ref)

    def finish(step, weights):
        at = pl.multiple_of(step * tile, tile)
        pre = jnp.dot(weights, normed_ref[...], preferred_element_type=jnp.float32)
        pre = pre + bias_ref[pl.ds(pl.multiple_of(offset + at, tile), tile), :]
        out_ref[pl.ds(at, tile), :] = jax.nn.gelu(pre, approximate=True).astype(jnp.bfloat16)

    def at_hand(step, carry):
        finish(step, block_ref[pl.ds(pl.multiple_of(step * tile, tile), tile), :])
        return carry

    def stream(step, carry):
        copy(step).wait()
        finish(step, buf[step - held])
        return carry

    if held:
        lax.fori_loop(0, held, at_hand, 0)
    lax.fori_loop(held, steps, stream, 0)
    if coming is not None:
        copy_next().wait()


def first_matmul(info, bias, w, offset, rows, block=None, coming=None, ahead=0, normed=None, gain=None, pieces=(), layout=None):
    tile = 256
    width, tokens = w.shape[2], bias.shape[1]
    held = 0 if block is None else block.shape[0] // tile
    streamed = rows // tile - held
    outs = [jax.ShapeDtypeStruct((rows, tokens), jnp.bfloat16)]
    if layout is None:
        args = [normed]
    else:
        args = [gain, *pieces]
        outs = [jax.ShapeDtypeStruct((width, tokens), jnp.bfloat16)] + outs
    if block is not None:
        args = [block, *args]
    if coming is not None:
        outs.append(jax.ShapeDtypeStruct((ahead, width), jnp.bfloat16))
    call = pallas(
        functools.partial(first_kernel, offset, held, coming, layout),
        outs,
        [SM, VM, ANY] + [VM] * len(args),
        [VM] * len(outs),
        [pltpu.VMEM((streamed, tile, width), jnp.bfloat16), pltpu.SemaphoreType.DMA((streamed + 1,))],
        flops=2 * rows * width * tokens,
        moved=2 * rows * width,
    )
    results = call(info, bias, w, *args)
    return results if len(outs) > 1 else results[0]


def pick_kernel(phase, info_ref, here_ref, crossed_ref, *outs):
    rows = outs[0].shape[0]

    @pl.when(info_ref[0] == phase)
    def _():
        for number, out_ref in enumerate(outs):
            out_ref[...] = here_ref[pl.ds(number * rows, rows), :]

    @pl.when(info_ref[0] != phase)
    def _():
        for number, out_ref in enumerate(outs):
            out_ref[...] = crossed_ref[pl.ds(number * rows, rows), :]


def pick(phase, info, here, crossed, count):
    out = jax.ShapeDtypeStruct((here.shape[0] // count, here.shape[1]), here.dtype)
    kernel = functools.partial(pick_kernel, phase)
    return pallas(kernel, [out] * count, [SM, VM, VM], [VM] * count, limit=8)(info, here, crossed)


def relay_kernel(info_ref, kept_ref, swapped_ref, out_ref, own_ref):
    half = own_ref.shape[0]

    @pl.when(info_ref[0] == 0)
    def _():
        out_ref[...] = kept_ref[...]
        own_ref[...] = kept_ref[:half]

    @pl.when(info_ref[0] != 0)
    def _():
        out_ref[...] = swapped_ref[...]
        own_ref[...] = swapped_ref[half:]


def relay(info, kept, swapped):
    half = (kept.shape[0] // 2, kept.shape[1])
    outs = [jax.ShapeDtypeStruct(kept.shape, kept.dtype), jax.ShapeDtypeStruct(half, kept.dtype)]
    return pallas(relay_kernel, outs, [SM, VM, VM], [VM, VM], limit=8)(info, kept, swapped)


def halve_kernel(front_ref, back_ref, lower_ref, upper_ref):
    mid = lower_ref.shape[0]
    lower_ref[...] = front_ref[:mid]
    upper_ref[...] = back_ref[mid:]


def halve(front, back):
    mid = front.shape[0] // 2
    outs = [
        jax.ShapeDtypeStruct((mid, front.shape[1]), front.dtype),
        jax.ShapeDtypeStruct((front.shape[0] - mid, front.shape[1]), front.dtype),
    ]
    return pallas(halve_kernel, outs, [VM, VM], [VM, VM], limit=8)(front, back)


def column_copies(info_ref, w_ref, buf, sems, places, t, tile):
    down = pl.ds(pl.multiple_of(t * tile, tile), tile)
    at = 0
    for i, (k, scale, row, rows) in enumerate(places):
        columns = pl.ds(pl.multiple_of(info_ref[1 + k] * scale + row, 128), rows)
        yield pltpu.make_async_copy(w_ref.at[0, down, columns], buf.at[down, pl.ds(at, rows)], sems.at[t, i])
        at += rows


def second_kernel(places, coming, held, first, ending, *refs):
    count = len(places)
    info_ref, w_ref = refs[:2]
    pieces, refs = refs[2 : 2 + count], refs[2 + count :]
    if held is not None:
        buf, refs = refs[0], refs[1:]
    if not first:
        acc_ref, refs = refs[0], refs[1:]
    if coming:
        next_sems, refs = refs[-1], refs[:-1]
    if held is None:
        buf, sems, refs = refs[-2], refs[-1], refs[:-2]
    joined, refs = refs[-1], refs[:-1]
    if coming:
        next_buf, refs = refs[-1], refs[:-1]
    depth, tile = w_ref.shape[1], 384
    tiles = depth // tile

    def start(t, carry):
        for copy in column_copies(info_ref, w_ref, buf, sems, places, t, tile):
            copy.start()
        return carry

    def start_next(t, carry):
        for copy in column_copies(info_ref, w_ref, next_buf, next_sems, coming, t, tile):
            copy.start()
        return carry

    def wait_next(t, carry):
        for copy in column_copies(info_ref, w_ref, next_buf, next_sems, coming, t, tile):
            copy.wait()
        return carry

    if held is None:
        lax.fori_loop(0, tiles, start, 0)
    if coming:
        lax.fori_loop(0, tiles, start_next, 0)
    at = 0
    for ref in pieces:
        joined[pl.ds(at, ref.shape[0]), :] = ref[...]
        at += ref.shape[0]
    span = pl.ds(0 if held is None else held, at)

    def body(t, carry):
        if held is None:
            for copy in column_copies(info_ref, w_ref, buf, sems, places, t, tile):
                copy.wait()
        own = pl.ds(pl.multiple_of(t * tile, tile), tile)
        acc = jnp.dot(buf[own, span], joined[...], preferred_element_type=jnp.float32)
        if not first:
            acc = acc_ref[own, :] + acc
        if not ending:
            refs[0][own, :] = acc
            return carry
        local_ref, bias_ref = refs[:2]
        result = local_ref[own, :].astype(jnp.float32) + (acc + bias_ref[own, :])
        if ending == 1:
            refs[2][own, :] = result.astype(jnp.bfloat16)
        else:
            early_ref, out_ref = refs[2:]
            rounded = result.astype(jnp.bfloat16).astype(jnp.float32)
            result = jnp.where(info_ref[0] == 0, early_ref[own, :].astype(jnp.float32), rounded)
            out_ref[:, own] = result.T.astype(jnp.bfloat16)
        return carry

    lax.fori_loop(0, tiles, body, 0)
    if coming:
        lax.fori_loop(0, tiles, wait_next, 0)


def second_matmul(info, acc, pieces, places, w, coming=(), buf=None, held=None, ends=()):
    depth, tokens = w.shape[1], pieces[0].shape[1]
    total = sum(piece.shape[0] for piece in pieces)
    ahead = sum(rows for *_, rows in coming)
    ending = max(0, len(ends) - 1)
    args = [info, w, *pieces]
    args += ([] if buf is None else [buf]) + ([] if acc is None else [acc]) + list(ends)
    if ending == 2:
        out = jax.ShapeDtypeStruct((tokens, depth), jnp.bfloat16)
    else:
        out = jax.ShapeDtypeStruct((depth, tokens), jnp.bfloat16 if ending else jnp.float32)
    outs, out_specs = [out], [VM]
    scratch = [pltpu.VMEM((total, tokens), jnp.bfloat16)]
    if buf is None:
        scratch += [
            pltpu.VMEM((depth, total), jnp.bfloat16),
            pltpu.SemaphoreType.DMA((depth // 384, len(pieces))),
        ]
    if coming:
        outs.append(jax.ShapeDtypeStruct((depth, ahead), jnp.bfloat16))
        out_specs.append(VM)
        scratch.append(pltpu.SemaphoreType.DMA((depth // 384, len(coming))))
    kernel = functools.partial(second_kernel, places, coming, held, acc is None, ending)
    cost = dict(flops=2 * depth * total * tokens, moved=2 * depth * total)
    call = pallas(kernel, outs, [SM, ANY] + [VM] * (len(args) - 2), out_specs, scratch, **cost)
    results = call(*args)
    return results if coming else results[0]


def ring_shards(ring, inputs, norm_gain, w_in, b_in, w_out, b_out):
    n = len(ring)
    last = n // 2
    tokens, part = inputs.shape[1:]
    half = part // 2
    width = norm_gain.shape[1]
    hidden = w_in.shape[1]
    side = hidden // 2
    seg = lax.axis_index("segment")
    place = {device: at for at, device in enumerate(ring)}
    behind = np.array([[ring[(place[t] - k) % n] for k in range(n)] for t in range(n)], np.int32)
    owner = jnp.asarray(behind)[lax.axis_index("tp")]
    info = jnp.concatenate([seg.reshape(1).astype(jnp.int32), owner])

    def hop(value, steps):
        return lax.ppermute(value, "tp", [(ring[at], ring[(at + steps) % n]) for at in range(n)])

    def swap(value):
        return lax.ppermute(value, "segment", [(0, 1), (1, 0)])

    def over_lanes(row):
        return jnp.broadcast_to(row[0][:, None], (row.shape[1], tokens))

    local = inputs[0].T
    own = lax.dynamic_slice_in_dim(inputs[0], seg * half, half, 1).T
    x_places = [(0, 0)] + [(k, 0) for step in range(1, last) for k in (step, n - step)] + [(last, 0)]

    early = None
    for phase in range(2):
        front = back = own
        mine, theirs = [own], [swap(own)]
        for step in range(1, last + 1):
            ready = front
            front, back = hop(front, 1), hop(back, -1) if step < last else None
            if phase == 0 and step == 1:
                front, back, info, local = lax.optimization_barrier((front, back, info, local))
            if phase == 0 and step == 2:
                _, gain = lax.optimization_barrier((ready, norm_gain))
                front, back, gain = lax.optimization_barrier((front, back, over_lanes(gain)))
            if phase == 0 and step == 3:
                _, bias_in, bias_out = lax.optimization_barrier((ready, b_in, b_out))
                front, back, bias_in, bias_out = lax.optimization_barrier(
                    (front, back, over_lanes(bias_in), over_lanes(bias_out))
                )
            mine += [front] if step == last else [front, back]
            theirs += [swap(front)] if step == last else [swap(front), swap(back)]
        ahead = side // 3
        layout = (part, half, x_places)
        normed, other, block = first_matmul(
            info, bias_in, w_in, side, side, coming=0, ahead=ahead, gain=gain, pieces=mine + theirs, layout=layout
        )
        crossed = swap(other)
        here = first_matmul(info, bias_in, w_in, 0, side, block=block, normed=normed)
        fronts = pick(phase, info, here, crossed, CHUNKS)
        backs = list(fronts)
        fronts = list(fronts)
        chunk = side // CHUNKS
        plans = [[(0, hidden, 0, side), (0, hidden, side, side)]]
        for step in range(1, last + 1):
            rows, at = (chunk // 2, chunk // 2) if step == last else (chunk, 0)
            plan = []
            for c in range(CHUNKS):
                plan += [(step, hidden, c * chunk, rows), (n - step, hidden, c * chunk + at, rows)]
            plans.append(plan + [(k, hidden, row + side, rows) for k, _, row, _ in plan])
        acc = buf = held = None
        pieces = [here, other]
        for step in range(1, last + 1):
            for c in range(CHUNKS):
                if step == last:
                    fronts[c], backs[c] = halve(fronts[c], backs[c])
                fronts[c], backs[c] = hop(fronts[c], 1), hop(backs[c], -1)
            acc, buf = second_matmul(info, acc, pieces, plans[step - 1], w_out, plans[step], buf, held)
            held = 0
            for c in range(CHUNKS):
                fronts[c], backs[c], _ = lax.optimization_barrier((fronts[c], backs[c], acc))
            pieces = [piece for pair in zip(fronts, backs) for piece in pair]
            pieces += [swap(piece) for piece in pieces]
        count = len(pieces) // 2
        acc = second_matmul(info, acc, pieces[:count], plans[last][:count], w_out, buf=buf, held=0)
        ends = [local, bias_out] + ([] if early is None else [early])
        result = second_matmul(info, acc, pieces[count:], plans[last][count:], w_out, buf=buf, held=side, ends=ends)
        if phase == 0:
            early = result
            local, own = relay(info, early, swap(early))
    return result.reshape(1, 1, tokens, part)


def snake(mesh):
    n = mesh.shape["tp"]
    return [2 * at for at in range(n // 2)] + [2 * at + 1 for at in reversed(range(n // 2))]


def solution(mesh):
    def shards(inputs, norm_gain, w_in, b_in, w_out, b_out):
        small = mesh.shape["tp"] == 8 and mesh.shape["segment"] == 2 and inputs.shape[0] == 1
        if small and inputs.shape[2] % 512 == 0 or small and inputs.shape[2] % 768 == 0:
            return ring_shards(snake(mesh), inputs, norm_gain, w_in, b_in, w_out, b_out)
        return plain_shards(inputs, norm_gain, w_in, b_in, w_out, b_out)

    return jax.shard_map(
        shards,
        mesh=mesh,
        in_specs=(
            P(None, "dp", "tp"),
            P("segment", None),
            P("segment", "tp", None),
            P("segment", "tp"),
            P("segment", "tp", None),
            P("segment", "tp"),
        ),
        out_specs=P("segment", None, "dp", "tp"),
        check_vma=False,
    )
```
